32 devices in a mesh: space: 16 (over z, x, core), traj: 2 (over y).
Axes of the slice: x: 2, y: 2, z: 4, core: 2. Of those that a mesh axis runs over, the one named last changes fastest.
Arguments:
- primal_init: float32 [32, 64, 96, 128], P('traj', 'space'), may hold values from -6 to 6
- adjoint_init: float32 [32, 64, 96, 128], P('traj', 'space'), may hold values from -6 to 6
- diffusion: float32 [3, 64, 96, 128], P(None, 'space'), may hold values from 0.03 to 0.15
- velocity: float32 [3, 64, 96, 128], P(None, 'space'), may hold values from -0.12 to 0.12
- sources: int32 [2, 32], P(None, 'traj'), may hold values from 0 to 786431
Outputs:
- gram: float32 [32, 32], P(None, 'traj')
The draws below stay inside these ranges and needn't reach their ends.
All inputs are finite; a program needn't handle non-finite values.
Results may differ from the reference program's by a relative error of at most 0.0003.
Values sent between devices are 32-bit elements; how exact they have to be, the bound alone decides.
A program may use at most 128 MiB of HBM per device.

```python
import math
import jax
import jax.numpy as jnp
from jax import lax

TRAJ = 32
NX = 96
NY = 128
STEPS = 4
IMPULSE = 1024
NZ = 64


def plant(entries, stream_key, smallest, largest):
    place = [jax.random.randint(jax.random.fold_in(stream_key, axis), (), 0, length) for axis, length in enumerate(entries.shape)]
    longest = entries.shape.index(max(entries.shape))
    beside = place[:longest] + [(place[longest] + 1) % entries.shape[longest]] + place[longest + 1:]
    return entries.at[tuple(place)].set(smallest).at[tuple(beside)].set(largest)


def level_of(rng, dims, shards, low, high):
    gain = 1.0
    for position, shards_of in shards:
        steps = jax.random.uniform(jax.random.fold_in(jax.random.fold_in(rng, 6), position), (shards_of,), jnp.float32, low / len(shards), high / len(shards))
        gain = gain * jnp.repeat(jnp.exp(steps), dims[position] // shards_of).reshape((-1,) + (1,) * (len(dims) - 1 - position))
    return gain


def normal_values(rng, dims, spread, limit, split=(), held_as=jnp.bfloat16):
    level = level_of(rng, dims, split, -0.22, 0.18) if split else 1.0
    entries = jax.random.normal(rng, dims, jnp.float32) * spread * level
    return jnp.minimum(jnp.maximum(entries, -limit), limit).astype(held_as)


def setup_inputs(seed: int = 0) -> dict:
    splits = jax.random.split(jax.random.key(seed), 6)
    return {
        "primal_init": normal_values(splits[0], (TRAJ, NZ, NX, NY), 1.0, 6.0, ((0, 2), (1, 16)), jnp.float32),
        "adjoint_init": normal_values(splits[1], (TRAJ, NZ, NX, NY), 1.0, 6.0, ((0, 2), (1, 16)), jnp.float32),
        "diffusion": jnp.clip(jnp.exp(math.log(0.15) - 1.609438 * jax.random.uniform(splits[2], (3, NZ, NX, NY), jnp.float32) ** level_of(splits[2], (3, NZ, NX, NY), ((1, 16),), -0.2, 0.2)), 0.03, 0.15),
        "velocity": jnp.clip(jax.random.uniform(splits[3], (3, NZ, NX, NY), jnp.float32, -0.12, 0.12) * level_of(splits[3], (3, NZ, NX, NY), ((1, 16),), -0.4, 0.0), -0.12, 0.12),
        "sources": plant(jax.random.randint(splits[4], (2, TRAJ), 0, NZ * NX * NY), jax.random.fold_in(splits[4], 1), 0, (NZ * NX * NY) - 1).astype(jnp.int32),
    }


def next_cell(values, along):
    length = values.shape[along]
    remainder = lax.slice_in_dim(values, 1, length, axis=along)
    boundary = jnp.zeros_like(lax.slice_in_dim(values, 0, 1, axis=along))
    return jnp.concatenate([remainder, boundary], axis=along)

def prev_cell(values, along):
    length = values.shape[along]
    remainder = lax.slice_in_dim(values, 0, length - 1, axis=along)
    boundary = jnp.zeros_like(lax.slice_in_dim(values, 0, 1, axis=along))
    return jnp.concatenate([boundary, remainder], axis=along)

def primal_update(current, plus_vals, minus_vals, outflow, inflow, out_below, in_below):
    summed = current
    for component in range(3):
        summed = summed + inflow[component] * plus_vals[component] - outflow[component] * current + out_below[component] * minus_vals[component] - in_below[component] * current
    return summed

def adjoint_update(current, plus_vals, minus_vals, outflow, in_below):
    summed = current
    for component in range(3):
        summed = summed + outflow[component] * (plus_vals[component] - current) + in_below[component] * (minus_vals[component] - current)
    return summed

def reference(primal_init, adjoint_init, diffusion, velocity, sources):
    outflow = diffusion + 0.5 * velocity
    inflow = diffusion - 0.5 * velocity
    out_below = [prev_cell(outflow[component], component) for component in range(3)]
    in_below = [prev_cell(inflow[component], component) for component in range(3)]
    flat_index = jnp.arange(NZ * NX * NY, dtype=jnp.int32).reshape(NZ, NX, NY)

    def run_primal(arguments):
        initial, source = arguments
        current = initial + (flat_index == source).astype(jnp.float32) * IMPULSE
        for step_index in range(STEPS):
            plus_vals = [next_cell(current, component) for component in range(3)]
            minus_vals = [prev_cell(current, component) for component in range(3)]
            current = primal_update(current, plus_vals, minus_vals, outflow, inflow, out_below, in_below)
        return current

    def run_adjoint(arguments):
        initial, source = arguments
        current = initial + (flat_index == source).astype(jnp.float32) * IMPULSE
        for step_index in range(STEPS):
            plus_vals = [next_cell(current, component) for component in range(3)]
            minus_vals = [prev_cell(current, component) for component in range(3)]
            current = adjoint_update(current, plus_vals, minus_vals, outflow, in_below)
        return current
    primal_final = lax.map(run_primal, (primal_init, sources[0]))
    adjoint_final = lax.map(run_adjoint, (adjoint_init, sources[1]))
    gram = lax.dot_general(adjoint_final.reshape(TRAJ, -1), primal_final.reshape(TRAJ, -1), (((1,), (1,)), ((), ())), precision=lax.Precision.HIGHEST, preferred_element_type=jnp.float32)
    return gram / math.sqrt(NZ * NX * NY)
```

```python
import functools
import math

import jax
import jax.numpy as jnp
from jax import lax
from jax.experimental import pallas as pl
from jax.experimental.pallas import tpu as pltpu
from jax.sharding import PartitionSpec as P

STEPS = 4
IMPULSE = 1024
GROUP = 4
CHUNK = 2
LAG = 3
EARLY = 1
MESH = pl.DeviceIdType.MESH


def coefficients(dv, coef, zz):
    rows, lanes = coef.shape[2:]
    row = lax.broadcasted_iota(jnp.int32, (rows, lanes), 0)
    lane = lax.broadcasted_iota(jnp.int32, (rows, lanes), 1)

    def faces(component, plane):
        d, v = dv[0, component, plane], dv[1, component, plane]
        return d + 0.5 * v, d - 0.5 * v

    out_z, in_z = faces(0, zz + 1)
    out_z_below, in_z_below = faces(0, zz)
    out_x, in_x = faces(1, zz + 1)
    out_y, in_y = faces(2, zz + 1)
    zero = jnp.zeros((rows, lanes), jnp.float32)
    below_x = lambda value: jnp.where(row == 0, zero, pltpu.roll(value, 1, 0))
    below_y = lambda value: jnp.where(lane == 0, zero, pltpu.roll(value, 1, 1))
    centre = out_z + in_z_below + out_x + below_x(in_x) + out_y + below_y(in_y)
    coef[0, zz] = 1.0 - centre
    coef[1, zz] = in_z
    coef[2, zz] = out_z_below
    coef[3, zz] = jnp.where(row == rows - 1, zero, in_x)
    coef[4, zz] = below_x(out_x)
    coef[5, zz] = jnp.where(lane == lanes - 1, zero, in_y)
    coef[6, zz] = below_y(out_y)


def kernel(
    dims,
    src_ref,
    p_ref,
    a_ref,
    d_ref,
    v_ref,
    out_ref,
    cur0,
    cur1,
    final,
    a_all,
    dv,
    coef,
    gred,
    part,
    part2,
    a_local,
    same_send,
    same_recv,
    cross_send,
    cross_recv,
    relay_send,
    relay_recv,
    below_send,
    below_recv,
    a_send,
    a_recv,
    in_send,
    in_recv,
    back_send,
    back_recv,
    up_send,
    up_recv,
    down_send,
    down_recv,
    red_send,
    red_recv,
    red2_send,
    red2_recv,
    go,
):
    n, n_traj, quad, size = dims
    fields, planes, rows, lanes = p_ref.shape
    half = fields // 2
    held = half // size
    deep = planes * 2
    steps = 2 * STEPS
    cur = (cur0, cur1)
    me = lax.axis_index("space")
    my_traj = lax.axis_index("traj")
    groups = n // quad
    mine, place = lax.div(me, quad), lax.rem(me, quad)
    hx, cx = lax.div(place, 2), lax.rem(place, 2)
    sibling = {"space": mine * quad + place + 1 - 2 * cx}
    crossing = {"space": mine * quad + 2 - hx}
    parity = lax.rem(my_traj, 2)
    partner = {"traj": my_traj + 1 - 2 * parity}
    stays = hx == cx
    relays = hx != cx
    first, last = mine == 0, mine == groups - 1
    has_up = jnp.logical_not(last & (cx == 1))
    has_down = jnp.logical_not(first & (cx == 0))
    above_id = {"space": jnp.minimum(me + 1 + 2 * cx, n - 1)}
    below_id = {"space": jnp.maximum(me - 3 + 2 * cx, 0)}

    def load_adjoint(f):
        return pltpu.make_async_copy(a_ref.at[f], a_all.at[my_traj, f], a_local.at[f])

    @pl.loop(0, fields)
    def _(f):
        load_adjoint(f).start()

    barrier = pltpu.get_barrier_semaphore()

    @pl.loop(1, n)
    def _(ahead):
        pl.semaphore_signal(
            barrier, inc=1, device_id={"space": lax.rem(me + ahead, n)}, device_id_type=MESH
        )

    for ahead in range(1, n_traj):
        pl.semaphore_signal(
            barrier,
            inc=1,
            device_id={"traj": lax.rem(my_traj + ahead, n_traj)},
            device_id_type=MESH,
        )
    pl.semaphore_wait(barrier, n - 1 + n_traj - 1)

    def remote(src, dst, send, recv, target):
        return pltpu.make_async_remote_copy(
            src_ref=src,
            dst_ref=dst,
            send_sem=send,
            recv_sem=recv,
            device_id=target,
            device_id_type=MESH,
        )

    pair = (d_ref, v_ref)

    def own_planes(block):
        return pl.ds(1 + planes * block, planes)

    def keep_faces(i):
        return pltpu.make_async_copy(pair[i], dv.at[i, :, own_planes(cx)], same_recv.at[i, cx])

    def give_faces(i, block):
        return remote(
            pair[i],
            dv.at[i, :, own_planes(block)],
            same_send.at[i],
            same_recv.at[i, block],
            sibling,
        )

    def cross_faces(i, a):
        return remote(
            pair[i].at[a],
            dv.at[i, a, own_planes(cx)],
            cross_send.at[a],
            cross_recv.at[cx, a],
            crossing,
        )

    def crossed_faces(a, block):
        face = dv.at[parity, a, own_planes(block)]
        return remote(face, face, cross_send.at[a], cross_recv.at[block, a], crossing)

    def relay_faces(a, block):
        face = dv.at[parity, a, own_planes(block)]
        return remote(face, face, relay_send.at[block, a], relay_recv.at[block, a], partner)

    def relayed_faces(a, block):
        face = dv.at[1 - parity, a, own_planes(block)]
        return remote(face, face, relay_send.at[block, a], relay_recv.at[block, a], partner)

    def keep_below(i):
        return pltpu.make_async_copy(pair[i].at[0, planes - 1], dv.at[i, 0, 0], below_recv.at[i])

    def give_below(i, k, target):
        return remote(
            pair[i].at[0, planes - 1],
            dv.at[i, 0, 0],
            below_send.at[i, k],
            below_recv.at[i],
            target,
        )

    side_id = {"space": mine * quad + 3}
    over_id = [{"space": jnp.minimum(mine + 1, groups - 1) * quad + 2 * k} for k in range(2)]

    def chunk_of(which, c):
        return pl.ds(which * half + c * size, size)

    def keep_start(c):
        return pltpu.make_async_copy(
            p_ref.at[chunk_of(hx, c)],
            cur0.at[pl.ds(c * size, size), own_planes(cx)],
            in_recv.at[c, cx],
        )

    def give_start(c, block):
        return remote(
            p_ref.at[chunk_of(hx, c)],
            cur0.at[pl.ds(c * size, size), own_planes(block)],
            in_send.at[c, 0],
            in_recv.at[c, block],
            sibling,
        )

    def cross_start(c, block):
        return remote(
            p_ref.at[chunk_of(1 - hx, c)],
            cur0.at[pl.ds(c * size, size), own_planes(block)],
            in_send.at[c, 1],
            in_recv.at[c, block],
            crossing,
        )

    for a in range(3):
        for i in range(2):

            @pl.when(parity == i)
            def _():
                cross_faces(i, a).start()

    @pl.when(place == 1)
    def _():
        for i in range(2):
            keep_below(i).start()
            give_below(i, 0, side_id).start()

    @pl.when((place == 3) & jnp.logical_not(last))
    def _():
        for i in range(2):
            for k in range(2):
                give_below(i, k, over_id[k]).start()

    @pl.when(stays)
    def _():
        for i in range(2):
            keep_faces(i).start()

        @pl.loop(0, held)
        def _(c):
            keep_start(c).start()

    @pl.when(relays)
    def _():
        for i in range(2):
            give_faces(i, cx).start()

        @pl.loop(0, held)
        def _(c):
            give_start(c, cx).start()

    @pl.loop(0, held)
    def _(c):
        cross_start(c, cx).start()

    grid = (rows, lanes)
    zero_plane = jnp.zeros(grid, jnp.float32)

    def with_impulse(value, source, plane):
        offset = lax.broadcasted_iota(jnp.int32, grid, 0) * lanes + lax.broadcasted_iota(
            jnp.int32, grid, 1
        )
        return value + jnp.where(offset == source - plane * (rows * lanes), float(IMPULSE), 0.0)

    def gather(ahead, f):
        return remote(
            a_all.at[my_traj, f],
            a_all.at[my_traj, f],
            a_send.at[ahead - 1, f],
            a_recv.at[ahead - 1, f],
            {"traj": lax.rem(my_traj + ahead, n_traj)},
        )

    def gathered(ahead, f):
        owner = lax.rem(my_traj + n_traj - ahead, n_traj)
        return remote(
            a_all.at[owner, f],
            a_all.at[owner, f],
            a_send.at[ahead - 1, f],
            a_recv.at[ahead - 1, f],
            {"traj": lax.rem(my_traj + ahead, n_traj)},
        )

    @pl.loop(0, fields)
    def _(f):
        load_adjoint(f).wait()
        for zz in range(planes):
            a_all[my_traj, f, zz] = with_impulse(
                a_all[my_traj, f, zz], src_ref[1, f], me * planes + zz
            )

        @pl.when((f >= 1) & (f <= EARLY))
        def _():
            for ahead in range(1, n_traj):
                gather(ahead, f - 1).start()

    @pl.when(first & (cx == 0))
    def _():
        for i in range(2):
            dv[i, 0, 0] = zero_plane

        @pl.loop(0, half)
        def _(f):
            for slot in range(2):
                cur[slot][f, 0] = zero_plane

    @pl.when(last & (cx == 1))
    def _():
        @pl.loop(0, half)
        def _(f):
            for slot in range(2):
                cur[slot][f, deep + 1] = zero_plane

    @pl.when(relays)
    def _():
        for a in range(3):
            for block in range(2):
                crossed_faces(a, block).wait_recv()
                relay_faces(a, block).start()
        pl.semaphore_signal(go, inc=1, device_id=sibling, device_id_type=MESH)

    @pl.when(stays)
    def _():
        for i in range(2):
            keep_faces(i).wait()
            give_faces(i, 1 - cx).wait_recv()
        pl.semaphore_wait(go, 1)

    @pl.loop(EARLY, fields)
    def _(f):
        for ahead in range(1, n_traj):
            gather(ahead, f).start()

    @pl.when(place == 1)
    def _():
        for i in range(2):
            keep_below(i).wait()

    @pl.when((place == 3) | ((cx == 0) & jnp.logical_not(first)))
    def _():
        for i in range(2):
            give_below(i, 0, side_id).wait_recv()

    @pl.when(relays)
    def _():
        for a in range(3):
            for block in range(2):
                relayed_faces(a, block).wait_recv()

    @pl.loop(0, deep)
    def _(zz):
        coefficients(dv, coef, zz)

    def halo_up(slot, c):
        return remote(
            cur[slot].at[pl.ds(c * size, size), deep],
            cur[slot].at[pl.ds(c * size, size), 0],
            up_send.at[slot, c],
            up_recv.at[slot, c],
            above_id,
        )

    def halo_down(slot, c):
        return remote(
            cur[slot].at[pl.ds(c * size, size), 1],
            cur[slot].at[pl.ds(c * size, size), deep + 1],
            down_send.at[slot, c],
            down_recv.at[slot, c],
            below_id,
        )

    def send_halos(slot, c):
        @pl.when(has_up)
        def _():
            halo_up(slot, c).start()

        @pl.when(has_down)
        def _():
            halo_down(slot, c).start()

    def wait_sent(slot, c):
        @pl.when(has_up)
        def _():
            halo_up(slot, c).wait_send()

        @pl.when(has_down)
        def _():
            halo_down(slot, c).wait_send()

    def wait_halos(slot, c):
        @pl.when(has_down)
        def _():
            halo_up(slot, c).wait_recv()

        @pl.when(has_up)
        def _():
            halo_down(slot, c).wait_recv()

    tiles = rows // 8

    def update(slot, c, zz):
        old, new = cur[slot], cur[1 - slot]
        for r in range(tiles):
            at = pl.ds(8 * r, 8)
            k = [coef[i, zz, at] for i in range(7)]
            for i in range(size):
                f = c * size + i
                p = old[f, zz + 1, at]
                if r > 0:
                    before = old[f, zz + 1, pl.ds(8 * r - 1, 8)]
                else:
                    before = pltpu.roll(p, 1, 0)
                if r < tiles - 1:
                    after = old[f, zz + 1, pl.ds(8 * r + 1, 8)]
                else:
                    after = pltpu.roll(p, 7, 0)
                new[f, zz + 1, at] = (
                    k[5] * pltpu.roll(p, lanes - 1, 1)
                    + k[6] * pltpu.roll(p, 1, 1)
                    + k[0] * p
                    + k[1] * old[f, zz + 2, at]
                    + k[2] * old[f, zz, at]
                    + k[3] * after
                    + k[4] * before
                )

    def add_impulses(c, zz):
        for i in range(size):
            f = c * size + i
            cur0[f, zz + 1] = with_impulse(
                cur0[f, zz + 1],
                src_ref[0, hx * half + f],
                (mine * 2 + cx) * deep + zz,
            )

    def wait_start(c):
        @pl.when(stays)
        def _():
            keep_start(c).wait()
            give_start(c, 1 - cx).wait_recv()

        @pl.when(relays)
        def _():
            for block in range(2):
                cross_start(c, block).wait_recv()

    def keep_final(c):
        return pltpu.make_async_copy(
            cur0.at[pl.ds(c * size, size), own_planes(cx)],
            final.at[chunk_of(hx, c)],
            back_recv.at[c, hx],
        )

    def give_final(c, b, which):
        return remote(
            cur0.at[pl.ds(c * size, size), own_planes(b)],
            final.at[chunk_of(which, c)],
            back_send.at[c, b],
            back_recv.at[c, which],
            {"space": mine * quad + cx * 2 + b},
        )

    @pl.loop(0, steps + 1 + (held - 1) * LAG)
    def _(turn):
        @pl.loop(0, held)
        def _(c):
            t = turn - c * LAG - 1

            @pl.when(t == -1)
            def _():
                wait_start(c)
                add_impulses(c, 0)
                add_impulses(c, deep - 1)
                send_halos(0, c)

                @pl.loop(1, deep - 1)
                def _(zz):
                    add_impulses(c, zz)

            for slot in range(2):

                @pl.when((t >= 0) & (t < steps) & (lax.rem(t, 2) == slot))
                def _():
                    @pl.when(t > 0)
                    def _():
                        wait_sent(1 - slot, c)

                    wait_halos(slot, c)

                    @pl.loop(0, 2)
                    def _(side):
                        update(slot, c, side * (deep - 1))

                    @pl.when(t < steps - 1)
                    def _():
                        send_halos(1 - slot, c)

                    @pl.loop(1, deep - 1)
                    def _(zz):
                        update(slot, c, zz)

            @pl.when(t == steps - 1)
            def _():
                @pl.when(stays)
                def _():
                    give_final(c, 1 - cx, hx).start()
                    keep_final(c).start()

                @pl.when(relays)
                def _():
                    for b in range(2):
                        give_final(c, b, hx).start()

    def wait_final(c):
        @pl.when(stays)
        def _():
            keep_final(c).wait()
            give_final(c, 1 - cx, 1 - hx).wait_recv()

        @pl.when(relays)
        def _():
            for which in range(2):
                give_final(c, 0, which).wait_recv()

    def gram_of(c, owner, kb):
        columns = [which * half + c * size + i for which in range(2) for i in range(size)]

        def plane(zz, sums):
            def tile(i, sums):
                at = pl.ds(pl.multiple_of(i * 8, 8), 8)
                left = [a_all[owner, kb * 4 + k, zz, at] for k in range(4)]
                right = [final[j, zz, at] for j in columns]
                return tuple(
                    sums[k * len(columns) + j] + left[k] * right[j]
                    for k in range(4)
                    for j in range(len(columns))
                )

            return lax.fori_loop(0, tiles, tile, sums, unroll=tiles)

        zero = jnp.zeros((8, lanes), jnp.float32)
        sums = lax.fori_loop(0, planes, plane, (zero,) * (4 * len(columns)))
        for k in range(4):
            for j, column in enumerate(columns):
                gred[owner * fields + kb * 4 + k, pl.ds(column, 1)] = jnp.sum(
                    sums[k * len(columns) + j], axis=0, keepdims=True
                )

    @pl.loop(0, held)
    def _(c):
        wait_final(c)

        @pl.loop(0, fields // 4)
        def _(kb):
            gram_of(c, my_traj, kb)

        for ahead in range(1, n_traj):

            @pl.loop(0, fields // 4)
            def _(kb):
                @pl.when(c == 0)
                def _():
                    for k in range(4):
                        gathered(ahead, kb * 4 + k).wait_recv()

                gram_of(c, lax.rem(my_traj + n_traj - ahead, n_traj), kb)

    part[place] = jnp.sum(gred[...], axis=-1)

    def inside(ahead):
        return pltpu.make_async_remote_copy(
            src_ref=part.at[place],
            dst_ref=part.at[place],
            send_sem=red_send.at[ahead - 1],
            recv_sem=red_recv.at[ahead - 1],
            device_id={"space": mine * quad + lax.rem(place + ahead, quad)},
            device_id_type=MESH,
        )

    for ahead in range(1, quad):
        inside(ahead).start()
    for ahead in range(1, quad):
        inside(ahead).wait_recv()
    value = part[0]
    for i in range(1, quad):
        value = value + part[i]
    part2[mine] = value

    def across(ahead):
        return pltpu.make_async_remote_copy(
            src_ref=part2.at[mine],
            dst_ref=part2.at[mine],
            send_sem=red2_send.at[ahead - 1],
            recv_sem=red2_recv.at[ahead - 1],
            device_id={"space": lax.rem(mine + ahead, groups) * quad + place},
            device_id_type=MESH,
        )

    for ahead in range(1, groups):
        across(ahead).start()
    for ahead in range(1, groups):
        across(ahead).wait_recv()
    value = part2[0]
    for i in range(1, groups):
        value = value + part2[i]
    out_ref[...] = value / math.sqrt(n * planes * rows * lanes)

    for ahead in range(1, quad):
        inside(ahead).wait_send()
    for ahead in range(1, groups):
        across(ahead).wait_send()

    @pl.loop(0, fields)
    def _(f):
        for ahead in range(1, n_traj):
            gather(ahead, f).wait_send()

    for a in range(3):
        crossed_faces(a, cx).wait_send()

    @pl.when(place == 1)
    def _():
        for i in range(2):
            give_below(i, 0, side_id).wait_send()

    @pl.when((place == 3) & jnp.logical_not(last))
    def _():
        for i in range(2):
            for k in range(2):
                give_below(i, k, over_id[k]).wait_send()

    @pl.when(relays)
    def _():
        for i in range(2):
            give_faces(i, cx).wait_send()
        for a in range(3):
            for block in range(2):
                relay_faces(a, block).wait_send()

    @pl.loop(0, held)
    def _(c):
        wait_sent(1, c)
        cross_start(c, cx).wait_send()

        @pl.when(stays)
        def _():
            give_final(c, 1 - cx, hx).wait_send()

        @pl.when(relays)
        def _():
            give_start(c, cx).wait_send()
            for b in range(2):
                give_final(c, b, hx).wait_send()


def solution(mesh):
    n, n_traj = mesh.shape["space"], mesh.shape["traj"]

    def on_device(primal_init, adjoint_init, diffusion, velocity, sources):
        fields, planes, rows, lanes = primal_init.shape
        quad = GROUP
        assert n % quad == 0 and n_traj % 2 == 0 and fields % (2 * CHUNK) == 0
        size = CHUNK
        half, deep = fields // 2, planes * 2
        held = half // size
        total = n_traj * fields
        hbm = pl.BlockSpec(memory_space=pltpu.HBM)
        dma = pltpu.SemaphoreType.DMA
        f32 = jnp.float32
        others = max(1, n_traj - 1)
        return pl.pallas_call(
            functools.partial(kernel, (n, n_traj, quad, size)),
            out_shape=jax.ShapeDtypeStruct((total, fields), f32),
            in_specs=[pl.BlockSpec(memory_space=pltpu.SMEM)] + [hbm] * 4,
            out_specs=pl.BlockSpec(memory_space=pltpu.VMEM),
            scratch_shapes=[
                *[pltpu.VMEM((half, deep + 2, rows, lanes), f32)] * 2,
                pltpu.VMEM((fields, planes, rows, lanes), f32),
                pltpu.VMEM((n_traj, fields, planes, rows, lanes), f32),
                pltpu.VMEM((2, 3, deep + 1, rows, lanes), f32),
                pltpu.VMEM((7, deep, rows, lanes), f32),
                pltpu.VMEM((total, fields, lanes), f32),
                pltpu.VMEM((quad, total, fields), f32),
                pltpu.VMEM((n // quad, total, fields), f32),
                dma((fields,)),
                dma((2,)),
                dma((2, 2)),
                dma((3,)),
                *[dma((2, 3))] * 3,
                dma((2, 2)),
                dma((2,)),
                *[dma((others, fields))] * 2,
                *[dma((held, 2))] * 4,
                *[dma((2, held))] * 4,
                *[dma((quad - 1,))] * 2,
                *[dma((max(1, n // quad - 1),))] * 2,
                pltpu.SemaphoreType.REGULAR,
            ],
            compiler_params=pltpu.CompilerParams(
                collective_id=0, has_side_effects=True, vmem_limit_bytes=67043328
            ),
        )(sources, primal_init, adjoint_init, diffusion, velocity)

    return jax.shard_map(
        on_device,
        mesh=mesh,
        in_specs=(
            P("traj", "space", None, None),
            P("traj", "space", None, None),
            P(None, "space", None, None),
            P(None, "space", None, None),
            P(None, "traj"),
        ),
        out_specs=P(None, "traj"),
        check_vma=False,
    )
```

```python
import functools
import math

import jax
import jax.numpy as jnp
from jax import lax
from jax.experimental import pallas as pl
from jax.experimental.pallas import tpu as pltpu
from jax.sharding import PartitionSpec as P

STEPS = 4
IMPULSE = 1024
GROUP = 4
CHUNK = 1
LAG = 1
EARLY = 1
MESH = pl.DeviceIdType.MESH


def coefficients(dv, coef, zz):
    rows, lanes = coef.shape[2:]
    row = lax.broadcasted_iota(jnp.int32, (rows, lanes), 0)
    lane = lax.broadcasted_iota(jnp.int32, (rows, lanes), 1)

    def faces(component, plane):
        d, v = dv[0, component, plane], dv[1, component, plane]
        return d + 0.5 * v, d - 0.5 * v

    out_z, in_z = faces(0, zz + 1)
    out_z_below, in_z_below = faces(0, zz)
    out_x, in_x = faces(1, zz + 1)
    out_y, in_y = faces(2, zz + 1)
    zero = jnp.zeros((rows, lanes), jnp.float32)
    below_x = lambda value: jnp.where(row == 0, zero, pltpu.roll(value, 1, 0))
    below_y = lambda value: jnp.where(lane == 0, zero, pltpu.roll(value, 1, 1))
    centre = out_z + in_z_below + out_x + below_x(in_x) + out_y + below_y(in_y)
    coef[0, zz] = 1.0 - centre
    coef[1, zz] = in_z
    coef[2, zz] = out_z_below
    coef[3, zz] = jnp.where(row == rows - 1, zero, in_x)
    coef[4, zz] = below_x(out_x)
    coef[5, zz] = jnp.where(lane == lanes - 1, zero, in_y)
    coef[6, zz] = below_y(out_y)


def kernel(
    dims,
    src_ref,
    p_ref,
    a_ref,
    d_ref,
    v_ref,
    out_ref,
    cur0,
    cur1,
    final,
    a_all,
    dv,
    coef,
    gred,
    part,
    part2,
    a_local,
    same_send,
    same_recv,
    cross_send,
    cross_recv,
    relay_send,
    relay_recv,
    below_send,
    below_recv,
    a_send,
    a_recv,
    in_send,
    in_recv,
    back_send,
    back_recv,
    up_send,
    up_recv,
    down_send,
    down_recv,
    red_send,
    red_recv,
    red2_send,
    red2_recv,
    go,
):
    n, n_traj, quad, size = dims
    fields, planes, rows, lanes = p_ref.shape
    half = fields // 2
    held = half // size
    deep = planes * 2
    steps = 2 * STEPS
    cur = (cur0, cur1)
    me = lax.axis_index("space")
    my_traj = lax.axis_index("traj")
    groups = n // quad
    mine, place = lax.div(me, quad), lax.rem(me, quad)
    hx, cx = lax.div(place, 2), lax.rem(place, 2)
    sibling = {"space": mine * quad + place + 1 - 2 * cx}
    crossing = {"space": mine * quad + 2 - hx}
    parity = lax.rem(my_traj, 2)
    partner = {"traj": my_traj + 1 - 2 * parity}
    stays = hx == cx
    relays = hx != cx
    first, last = mine == 0, mine == groups - 1
    has_up = jnp.logical_not(last & (cx == 1))
    has_down = jnp.logical_not(first & (cx == 0))
    above_id = {"space": jnp.minimum(me + 1 + 2 * cx, n - 1)}
    below_id = {"space": jnp.maximum(me - 3 + 2 * cx, 0)}

    def load_adjoint(f):
        return pltpu.make_async_copy(a_ref.at[f], a_all.at[my_traj, f], a_local.at[f])

    @pl.loop(0, fields)
    def _(f):
        load_adjoint(f).start()

    barrier = pltpu.get_barrier_semaphore()

    @pl.loop(1, n)
    def _(ahead):
        pl.semaphore_signal(
            barrier, inc=1, device_id={"space": lax.rem(me + ahead, n)}, device_id_type=MESH
        )

    for ahead in range(1, n_traj):
        pl.semaphore_signal(
            barrier,
            inc=1,
            device_id={"traj": lax.rem(my_traj + ahead, n_traj)},
            device_id_type=MESH,
        )
    pl.semaphore_wait(barrier, n - 1 + n_traj - 1)

    def remote(src, dst, send, recv, target):
        return pltpu.make_async_remote_copy(
            src_ref=src,
            dst_ref=dst,
            send_sem=send,
            recv_sem=recv,
            device_id=target,
            device_id_type=MESH,
        )

    pair = (d_ref, v_ref)

    def own_planes(block):
        return pl.ds(1 + planes * block, planes)

    def keep_faces(i):
        return pltpu.make_async_copy(pair[i], dv.at[i, :, own_planes(cx)], same_recv.at[i, cx])

    def give_faces(i, block):
        return remote(
            pair[i],
            dv.at[i, :, own_planes(block)],
            same_send.at[i],
            same_recv.at[i, block],
            sibling,
        )

    def cross_faces(i, a):
        return remote(
            pair[i].at[a],
            dv.at[i, a, own_planes(cx)],
            cross_send.at[a],
            cross_recv.at[cx, a],
            crossing,
        )

    def crossed_faces(a, block):
        face = dv.at[parity, a, own_planes(block)]
        return remote(face, face, cross_send.at[a], cross_recv.at[block, a], crossing)

    def relay_faces(a, block):
        face = dv.at[parity, a, own_planes(block)]
        return remote(face, face, relay_send.at[block, a], relay_recv.at[block, a], partner)

    def relayed_faces(a, block):
        face = dv.at[1 - parity, a, own_planes(block)]
        return remote(face, face, relay_send.at[block, a], relay_recv.at[block, a], partner)

    def keep_below(i):
        return pltpu.make_async_copy(pair[i].at[0, planes - 1], dv.at[i, 0, 0], below_recv.at[i])

    def give_below(i, k, target):
        return remote(
            pair[i].at[0, planes - 1],
            dv.at[i, 0, 0],
            below_send.at[i, k],
            below_recv.at[i],
            target,
        )

    side_id = {"space": mine * quad + 3}
    over_id = [{"space": jnp.minimum(mine + 1, groups - 1) * quad + 2 * k} for k in range(2)]

    def chunk_of(which, c):
        return pl.ds(which * half + c * size, size)

    def keep_start(c):
        return pltpu.make_async_copy(
            p_ref.at[chunk_of(hx, c)],
            cur0.at[pl.ds(c * size, size), own_planes(cx)],
            in_recv.at[c, cx],
        )

    def give_start(c, block):
        return remote(
            p_ref.at[chunk_of(hx, c)],
            cur0.at[pl.ds(c * size, size), own_planes(block)],
            in_send.at[c, 0],
            in_recv.at[c, block],
            sibling,
        )

    def cross_start(c, block):
        return remote(
            p_ref.at[chunk_of(1 - hx, c)],
            cur0.at[pl.ds(c * size, size), own_planes(block)],
            in_send.at[c, 1],
            in_recv.at[c, block],
            crossing,
        )

    for a in range(3):
        for i in range(2):

            @pl.when(parity == i)
            def _():
                cross_faces(i, a).start()

    @pl.when(place == 1)
    def _():
        for i in range(2):
            keep_below(i).start()
            give_below(i, 0, side_id).start()

    @pl.when((place == 3) & jnp.logical_not(last))
    def _():
        for i in range(2):
            for k in range(2):
                give_below(i, k, over_id[k]).start()

    @pl.when(stays)
    def _():
        for i in range(2):
            keep_faces(i).start()

        @pl.loop(0, held)
        def _(c):
            keep_start(c).start()

    @pl.when(relays)
    def _():
        for i in range(2):
            give_faces(i, cx).start()

        @pl.loop(0, held)
        def _(c):
            give_start(c, cx).start()

    @pl.loop(0, held)
    def _(c):
        cross_start(c, cx).start()

    grid = (rows, lanes)
    zero_plane = jnp.zeros(grid, jnp.float32)

    def with_impulse(value, source, plane):
        offset = lax.broadcasted_iota(jnp.int32, grid, 0) * lanes + lax.broadcasted_iota(
            jnp.int32, grid, 1
        )
        return value + jnp.where(offset == source - plane * (rows * lanes), float(IMPULSE), 0.0)

    def gather(ahead, f):
        return remote(
            a_all.at[my_traj, f],
            a_all.at[my_traj, f],
            a_send.at[ahead - 1, f],
            a_recv.at[ahead - 1, f],
            {"traj": lax.rem(my_traj + ahead, n_traj)},
        )

    def gathered(ahead, f):
        owner = lax.rem(my_traj + n_traj - ahead, n_traj)
        return remote(
            a_all.at[owner, f],
            a_all.at[owner, f],
            a_send.at[ahead - 1, f],
            a_recv.at[ahead - 1, f],
            {"traj": lax.rem(my_traj + ahead, n_traj)},
        )

    @pl.loop(0, fields)
    def _(f):
        load_adjoint(f).wait()
        for zz in range(planes):
            a_all[my_traj, f, zz] = with_impulse(
                a_all[my_traj, f, zz], src_ref[1, f], me * planes + zz
            )

        @pl.when((f >= 1) & (f <= EARLY))
        def _():
            for ahead in range(1, n_traj):
                gather(ahead, f - 1).start()

    @pl.when(first & (cx == 0))
    def _():
        for i in range(2):
            dv[i, 0, 0] = zero_plane

        @pl.loop(0, half)
        def _(f):
            for slot in range(2):
                cur[slot][f, 0] = zero_plane

    @pl.when(last & (cx == 1))
    def _():
        @pl.loop(0, half)
        def _(f):
            for slot in range(2):
                cur[slot][f, deep + 1] = zero_plane

    @pl.when(relays)
    def _():
        for a in range(3):
            for block in range(2):
                crossed_faces(a, block).wait_recv()
                relay_faces(a, block).start()
        pl.semaphore_signal(go, inc=1, device_id=sibling, device_id_type=MESH)

    @pl.when(stays)
    def _():
        for i in range(2):
            keep_faces(i).wait()
            give_faces(i, 1 - cx).wait_recv()
        pl.semaphore_wait(go, 1)

    @pl.loop(EARLY, fields)
    def _(f):
        for ahead in range(1, n_traj):
            gather(ahead, f).start()

    @pl.when(place == 1)
    def _():
        for i in range(2):
            keep_below(i).wait()

    @pl.when((place == 3) | ((cx == 0) & jnp.logical_not(first)))
    def _():
        for i in range(2):
            give_below(i, 0, side_id).wait_recv()

    @pl.when(relays)
    def _():
        for a in range(3):
            for block in range(2):
                relayed_faces(a, block).wait_recv()

    @pl.loop(0, deep)
    def _(zz):
        coefficients(dv, coef, zz)

    def halo_up(slot, c):
        return remote(
            cur[slot].at[pl.ds(c * size, size), deep],
            cur[slot].at[pl.ds(c * size, size), 0],
            up_send.at[slot, c],
            up_recv.at[slot, c],
            above_id,
        )

    def halo_down(slot, c):
        return remote(
            cur[slot].at[pl.ds(c * size, size), 1],
            cur[slot].at[pl.ds(c * size, size), deep + 1],
            down_send.at[slot, c],
            down_recv.at[slot, c],
            below_id,
        )

    def send_halos(slot, c):
        @pl.when(has_up)
        def _():
            halo_up(slot, c).start()

        @pl.when(has_down)
        def _():
            halo_down(slot, c).start()

    def wait_sent(slot, c):
        @pl.when(has_up)
        def _():
            halo_up(slot, c).wait_send()

        @pl.when(has_down)
        def _():
            halo_down(slot, c).wait_send()

    def wait_halos(slot, c):
        @pl.when(has_down)
        def _():
            halo_up(slot, c).wait_recv()

        @pl.when(has_up)
        def _():
            halo_down(slot, c).wait_recv()

    tiles = rows // 8

    def update(slot, c, zs):
        old, new = cur[slot], cur[1 - slot]
        for r in range(tiles):
            at = pl.ds(8 * r, 8)
            for f in [c * size + i for i in range(size)]:
                for zz in zs:
                    k = [coef[i, zz, at] for i in range(7)]
                    p = old[f, zz + 1, at]
                    if r > 0:
                        before = old[f, zz + 1, pl.ds(8 * r - 1, 8)]
                    else:
                        before = pltpu.roll(p, 1, 0)
                    if r < tiles - 1:
                        after = old[f, zz + 1, pl.ds(8 * r + 1, 8)]
                    else:
                        after = pltpu.roll(p, 7, 0)
                    new[f, zz + 1, at] = (
                        k[5] * pltpu.roll(p, lanes - 1, 1)
                        + k[6] * pltpu.roll(p, 1, 1)
                        + k[0] * p
                        + k[1] * old[f, zz + 2, at]
                        + k[2] * old[f, zz, at]
                        + k[3] * after
                        + k[4] * before
                    )

    def add_impulses(c, zz):
        for i in range(size):
            f = c * size + i
            cur0[f, zz + 1] = with_impulse(
                cur0[f, zz + 1],
                src_ref[0, hx * half + f],
                (mine * 2 + cx) * deep + zz,
            )

    def wait_start(c):
        @pl.when(stays)
        def _():
            keep_start(c).wait()
            give_start(c, 1 - cx).wait_recv()

        @pl.when(relays)
        def _():
            for block in range(2):
                cross_start(c, block).wait_recv()

    def keep_final(c):
        return pltpu.make_async_copy(
            cur0.at[pl.ds(c * size, size), own_planes(cx)],
            final.at[chunk_of(hx, c)],
            back_recv.at[c, hx],
        )

    def give_final(c, b, which):
        return remote(
            cur0.at[pl.ds(c * size, size), own_planes(b)],
            final.at[chunk_of(which, c)],
            back_send.at[c, b],
            back_recv.at[c, which],
            {"space": mine * quad + cx * 2 + b},
        )

    @pl.loop(0, steps + 1 + (held - 1) * LAG)
    def _(turn):
        @pl.loop(0, held)
        def _(c):
            t = turn - c * LAG - 1

            @pl.when(t == -1)
            def _():
                wait_start(c)
                add_impulses(c, 0)
                add_impulses(c, deep - 1)
                send_halos(0, c)

                @pl.loop(1, deep - 1)
                def _(zz):
                    add_impulses(c, zz)

            for slot in range(2):

                @pl.when((t >= 0) & (t < steps) & (lax.rem(t, 2) == slot))
                def _():
                    @pl.when(t > 0)
                    def _():
                        wait_sent(1 - slot, c)

                    wait_halos(slot, c)

                    update(slot, c, (0, deep - 1))

                    @pl.when(t < steps - 1)
                    def _():
                        send_halos(1 - slot, c)

                    @pl.loop(1, deep - 1, step=2)
                    def _(zz):
                        update(slot, c, (zz, zz + 1))

            @pl.when(t == steps - 1)
            def _():
                @pl.when(stays)
                def _():
                    give_final(c, 1 - cx, hx).start()
                    keep_final(c).start()

                @pl.when(relays)
                def _():
                    for b in range(2):
                        give_final(c, b, hx).start()

    def wait_final(c):
        @pl.when(stays)
        def _():
            keep_final(c).wait()
            give_final(c, 1 - cx, 1 - hx).wait_recv()

        @pl.when(relays)
        def _():
            for which in range(2):
                give_final(c, 0, which).wait_recv()

    def gram_of(c, owner, kb):
        columns = [which * half + c * size + i for which in range(2) for i in range(size)]

        def plane(zz, sums):
            def tile(i, sums):
                at = pl.ds(pl.multiple_of(i * 8, 8), 8)
                left = [a_all[owner, kb * 4 + k, zz, at] for k in range(4)]
                right = [final[j, zz, at] for j in columns]
                return tuple(
                    sums[k * len(columns) + j] + left[k] * right[j]
                    for k in range(4)
                    for j in range(len(columns))
                )

            return lax.fori_loop(0, tiles, tile, sums, unroll=tiles)

        zero = jnp.zeros((8, lanes), jnp.float32)
        sums = lax.fori_loop(0, planes, plane, (zero,) * (4 * len(columns)))
        for k in range(4):
            for j, column in enumerate(columns):
                gred[owner * fields + kb * 4 + k, pl.ds(column, 1)] = jnp.sum(
                    sums[k * len(columns) + j], axis=0, keepdims=True
                )

    blocks = fields // 4

    def gram_own(c):
        @pl.loop(0, blocks)
        def _(kb):
            gram_of(c, my_traj, kb)

    def gram_other(ahead, c, kb):
        gram_of(c, lax.rem(my_traj + n_traj - ahead, n_traj), kb)

    def wait_block(ahead, kb):
        for k in range(4):
            gathered(ahead, kb * 4 + k).wait_recv()

    @pl.loop(0, held - 1)
    def _(c):
        wait_final(c)
        gram_own(c)
        for ahead in range(1, n_traj):

            @pl.loop(0, blocks - 1)
            def _(kb):
                @pl.when(c == 0)
                def _():
                    wait_block(ahead, kb)

                gram_other(ahead, c, kb)

    for ahead in range(1, n_traj):
        wait_block(ahead, blocks - 1)

    @pl.loop(0, held - 1)
    def _(c):
        for ahead in range(1, n_traj):
            gram_other(ahead, c, blocks - 1)

    wait_final(held - 1)
    gram_own(held - 1)
    for ahead in range(1, n_traj):

        @pl.loop(0, blocks)
        def _(kb):
            gram_other(ahead, held - 1, kb)

    part[place] = jnp.sum(gred[...], axis=-1)

    def inside(ahead):
        return pltpu.make_async_remote_copy(
            src_ref=part.at[place],
            dst_ref=part.at[place],
            send_sem=red_send.at[ahead - 1],
            recv_sem=red_recv.at[ahead - 1],
            device_id={"space": mine * quad + lax.rem(place + ahead, quad)},
            device_id_type=MESH,
        )

    for ahead in range(1, quad):
        inside(ahead).start()
    for ahead in range(1, quad):
        inside(ahead).wait_recv()
    value = part[0]
    for i in range(1, quad):
        value = value + part[i]
    part2[mine] = value

    def across(ahead):
        return pltpu.make_async_remote_copy(
            src_ref=part2.at[mine],
            dst_ref=part2.at[mine],
            send_sem=red2_send.at[ahead - 1],
            recv_sem=red2_recv.at[ahead - 1],
            device_id={"space": lax.rem(mine + ahead, groups) * quad + place},
            device_id_type=MESH,
        )

    for ahead in range(1, groups):
        across(ahead).start()
    for ahead in range(1, groups):
        across(ahead).wait_recv()
    value = part2[0]
    for i in range(1, groups):
        value = value + part2[i]
    out_ref[...] = value / math.sqrt(n * planes * rows * lanes)

    for ahead in range(1, quad):
        inside(ahead).wait_send()
    for ahead in range(1, groups):
        across(ahead).wait_send()

    @pl.loop(0, fields)
    def _(f):
        for ahead in range(1, n_traj):
            gather(ahead, f).wait_send()

    for a in range(3):
        crossed_faces(a, cx).wait_send()

    @pl.when(place == 1)
    def _():
        for i in range(2):
            give_below(i, 0, side_id).wait_send()

    @pl.when((place == 3) & jnp.logical_not(last))
    def _():
        for i in range(2):
            for k in range(2):
                give_below(i, k, over_id[k]).wait_send()

    @pl.when(relays)
    def _():
        for i in range(2):
            give_faces(i, cx).wait_send()
        for a in range(3):
            for block in range(2):
                relay_faces(a, block).wait_send()

    @pl.loop(0, held)
    def _(c):
        wait_sent(1, c)
        cross_start(c, cx).wait_send()

        @pl.when(stays)
        def _():
            give_final(c, 1 - cx, hx).wait_send()

        @pl.when(relays)
        def _():
            give_start(c, cx).wait_send()
            for b in range(2):
                give_final(c, b, hx).wait_send()


def solution(mesh):
    n, n_traj = mesh.shape["space"], mesh.shape["traj"]

    def on_device(primal_init, adjoint_init, diffusion, velocity, sources):
        fields, planes, rows, lanes = primal_init.shape
        quad = GROUP
        assert n % quad == 0 and n_traj % 2 == 0 and fields % (4 * CHUNK) == 0
        size = CHUNK
        half, deep = fields // 2, planes * 2
        held = half // size
        total = n_traj * fields
        hbm = pl.BlockSpec(memory_space=pltpu.HBM)
        dma = pltpu.SemaphoreType.DMA
        f32 = jnp.float32
        others = max(1, n_traj - 1)
        return pl.pallas_call(
            functools.partial(kernel, (n, n_traj, quad, size)),
            out_shape=jax.ShapeDtypeStruct((total, fields), f32),
            in_specs=[pl.BlockSpec(memory_space=pltpu.SMEM)] + [hbm] * 4,
            out_specs=pl.BlockSpec(memory_space=pltpu.VMEM),
            scratch_shapes=[
                *[pltpu.VMEM((half, deep + 2, rows, lanes), f32)] * 2,
                pltpu.VMEM((fields, planes, rows, lanes), f32),
                pltpu.VMEM((n_traj, fields, planes, rows, lanes), f32),
                pltpu.VMEM((2, 3, deep + 1, rows, lanes), f32),
                pltpu.VMEM((7, deep, rows, lanes), f32),
                pltpu.VMEM((total, fields, lanes), f32),
                pltpu.VMEM((quad, total, fields), f32),
                pltpu.VMEM((n // quad, total, fields), f32),
                dma((fields,)),
                dma((2,)),
                dma((2, 2)),
                dma((3,)),
                *[dma((2, 3))] * 3,
                dma((2, 2)),
                dma((2,)),
                *[dma((others, fields))] * 2,
                *[dma((held, 2))] * 4,
                *[dma((2, held))] * 4,
                *[dma((quad - 1,))] * 2,
                *[dma((max(1, n // quad - 1),))] * 2,
                pltpu.SemaphoreType.REGULAR,
            ],
            compiler_params=pltpu.CompilerParams(
                collective_id=0, has_side_effects=True, vmem_limit_bytes=67043328
            ),
        )(sources, primal_init, adjoint_init, diffusion, velocity)

    return jax.shard_map(
        on_device,
        mesh=mesh,
        in_specs=(
            P("traj", "space", None, None),
            P("traj", "space", None, None),
            P(None, "space", None, None),
            P(None, "space", None, None),
            P(None, "traj"),
        ),
        out_specs=P(None, "traj"),
        check_vma=False,
    )
```

```python
import functools
import math

import jax
import jax.numpy as jnp
from jax import lax
from jax.experimental import pallas as pl
from jax.experimental.pallas import tpu as pltpu
from jax.sharding import PartitionSpec as P

STEPS = 4
IMPULSE = 1024
GROUP = 4
CHUNK = 1
LAG = 1
EARLY = 1
MESH = pl.DeviceIdType.MESH


def coefficients(dv, coef, zz):
    rows, lanes = coef.shape[2:]
    row = lax.broadcasted_iota(jnp.int32, (rows, lanes), 0)
    lane = lax.broadcasted_iota(jnp.int32, (rows, lanes), 1)

    def faces(component, plane):
        d, v = dv[0, component, plane], dv[1, component, plane]
        return d + 0.5 * v, d - 0.5 * v

    out_z, in_z = faces(0, zz + 1)
    out_z_below, in_z_below = faces(0, zz)
    out_x, in_x = faces(1, zz + 1)
    out_y, in_y = faces(2, zz + 1)
    zero = jnp.zeros((rows, lanes), jnp.float32)
    below_x = lambda value: jnp.where(row == 0, zero, pltpu.roll(value, 1, 0))
    below_y = lambda value: jnp.where(lane == 0, zero, pltpu.roll(value, 1, 1))
    centre = out_z + in_z_below + out_x + below_x(in_x) + out_y + below_y(in_y)
    coef[0, zz] = 1.0 - centre
    coef[1, zz] = in_z
    coef[2, zz] = out_z_below
    coef[3, zz] = jnp.where(row == rows - 1, zero, in_x)
    coef[4, zz] = below_x(out_x)
    coef[5, zz] = jnp.where(lane == lanes - 1, zero, in_y)
    coef[6, zz] = below_y(out_y)


def kernel(
    dims,
    src_ref,
    p_ref,
    a_ref,
    d_ref,
    v_ref,
    out_ref,
    cur0,
    cur1,
    final,
    a_all,
    dv,
    coef,
    gred,
    box,
    part,
    a_local,
    same_send,
    same_recv,
    cross_send,
    cross_recv,
    relay_send,
    relay_recv,
    below_send,
    below_recv,
    a_send,
    a_recv,
    in_send,
    in_recv,
    back_send,
    back_recv,
    up_send,
    up_recv,
    down_send,
    down_recv,
    red_send,
    red_recv,
    go,
):
    n, n_traj, quad, size = dims
    fields, planes, rows, lanes = p_ref.shape
    half = fields // 2
    held = half // size
    deep = planes * 2
    steps = 2 * STEPS
    cur = (cur0, cur1)
    me = lax.axis_index("space")
    my_traj = lax.axis_index("traj")
    groups = n // quad
    mine, place = lax.div(me, quad), lax.rem(me, quad)
    hx, cx = lax.div(place, 2), lax.rem(place, 2)
    sibling = {"space": mine * quad + place + 1 - 2 * cx}
    crossing = {"space": mine * quad + 2 - hx}
    parity = lax.rem(my_traj, 2)
    partner = {"traj": my_traj + 1 - 2 * parity}
    stays = hx == cx
    relays = hx != cx
    first, last = mine == 0, mine == groups - 1
    has_up = jnp.logical_not(last & (cx == 1))
    has_down = jnp.logical_not(first & (cx == 0))
    above_id = {"space": jnp.minimum(me + 1 + 2 * cx, n - 1)}
    below_id = {"space": jnp.maximum(me - 3 + 2 * cx, 0)}

    def load_adjoint(f):
        return pltpu.make_async_copy(a_ref.at[f], a_all.at[my_traj, f], a_local.at[f])

    @pl.loop(0, fields)
    def _(f):
        load_adjoint(f).start()

    barrier = pltpu.get_barrier_semaphore()

    @pl.loop(1, n)
    def _(ahead):
        pl.semaphore_signal(
            barrier, inc=1, device_id={"space": lax.rem(me + ahead, n)}, device_id_type=MESH
        )

    for ahead in range(1, n_traj):
        pl.semaphore_signal(
            barrier,
            inc=1,
            device_id={"traj": lax.rem(my_traj + ahead, n_traj)},
            device_id_type=MESH,
        )
    pl.semaphore_wait(barrier, n - 1 + n_traj - 1)

    def remote(src, dst, send, recv, target):
        return pltpu.make_async_remote_copy(
            src_ref=src,
            dst_ref=dst,
            send_sem=send,
            recv_sem=recv,
            device_id=target,
            device_id_type=MESH,
        )

    pair = (d_ref, v_ref)

    def own_planes(block):
        return pl.ds(1 + planes * block, planes)

    def keep_faces(i):
        return pltpu.make_async_copy(pair[i], dv.at[i, :, own_planes(cx)], same_recv.at[i, cx])

    def give_faces(i, block):
        return remote(
            pair[i],
            dv.at[i, :, own_planes(block)],
            same_send.at[i],
            same_recv.at[i, block],
            sibling,
        )

    def cross_faces(i, a):
        return remote(
            pair[i].at[a],
            dv.at[i, a, own_planes(cx)],
            cross_send.at[a],
            cross_recv.at[cx, a],
            crossing,
        )

    def crossed_faces(a, block):
        face = dv.at[parity, a, own_planes(block)]
        return remote(face, face, cross_send.at[a], cross_recv.at[block, a], crossing)

    def relay_faces(a, block):
        face = dv.at[parity, a, own_planes(block)]
        return remote(face, face, relay_send.at[block, a], relay_recv.at[block, a], partner)

    def relayed_faces(a, block):
        face = dv.at[1 - parity, a, own_planes(block)]
        return remote(face, face, relay_send.at[block, a], relay_recv.at[block, a], partner)

    def keep_below(i):
        return pltpu.make_async_copy(pair[i].at[0, planes - 1], dv.at[i, 0, 0], below_recv.at[i])

    def give_below(i, k, target):
        return remote(
            pair[i].at[0, planes - 1],
            dv.at[i, 0, 0],
            below_send.at[i, k],
            below_recv.at[i],
            target,
        )

    side_id = {"space": mine * quad + 3}
    over_id = [{"space": jnp.minimum(mine + 1, groups - 1) * quad + 2 * k} for k in range(2)]

    def chunk_of(which, c):
        return pl.ds(which * half + c * size, size)

    def keep_start(c):
        return pltpu.make_async_copy(
            p_ref.at[chunk_of(hx, c)],
            cur0.at[pl.ds(c * size, size), own_planes(cx)],
            in_recv.at[c, cx],
        )

    def give_start(c, block):
        return remote(
            p_ref.at[chunk_of(hx, c)],
            cur0.at[pl.ds(c * size, size), own_planes(block)],
            in_send.at[c, 0],
            in_recv.at[c, block],
            sibling,
        )

    def cross_start(c, block):
        return remote(
            p_ref.at[chunk_of(1 - hx, c)],
            cur0.at[pl.ds(c * size, size), own_planes(block)],
            in_send.at[c, 1],
            in_recv.at[c, block],
            crossing,
        )

    for a in range(3):
        for i in range(2):

            @pl.when(parity == i)
            def _():
                cross_faces(i, a).start()

    @pl.when(place == 1)
    def _():
        for i in range(2):
            keep_below(i).start()
            give_below(i, 0, side_id).start()

    @pl.when((place == 3) & jnp.logical_not(last))
    def _():
        for i in range(2):
            for k in range(2):
                give_below(i, k, over_id[k]).start()

    @pl.when(stays)
    def _():
        for i in range(2):
            keep_faces(i).start()

        @pl.loop(0, held)
        def _(c):
            keep_start(c).start()

    @pl.when(relays)
    def _():
        for i in range(2):
            give_faces(i, cx).start()

        @pl.loop(0, held)
        def _(c):
            give_start(c, cx).start()

    @pl.loop(0, held)
    def _(c):
        cross_start(c, cx).start()

    grid = (rows, lanes)
    zero_plane = jnp.zeros(grid, jnp.float32)

    def with_impulse(value, source, plane):
        offset = lax.broadcasted_iota(jnp.int32, grid, 0) * lanes + lax.broadcasted_iota(
            jnp.int32, grid, 1
        )
        return value + jnp.where(offset == source - plane * (rows * lanes), float(IMPULSE), 0.0)

    def gather(ahead, f):
        return remote(
            a_all.at[my_traj, f],
            a_all.at[my_traj, f],
            a_send.at[ahead - 1, f],
            a_recv.at[ahead - 1, f],
            {"traj": lax.rem(my_traj + ahead, n_traj)},
        )

    def gathered(ahead, f):
        owner = lax.rem(my_traj + n_traj - ahead, n_traj)
        return remote(
            a_all.at[owner, f],
            a_all.at[owner, f],
            a_send.at[ahead - 1, f],
            a_recv.at[ahead - 1, f],
            {"traj": lax.rem(my_traj + ahead, n_traj)},
        )

    @pl.loop(0, fields)
    def _(f):
        load_adjoint(f).wait()
        for zz in range(planes):
            a_all[my_traj, f, zz] = with_impulse(
                a_all[my_traj, f, zz], src_ref[1, f], me * planes + zz
            )

        @pl.when((f >= 1) & (f <= EARLY))
        def _():
            for ahead in range(1, n_traj):
                gather(ahead, f - 1).start()

    @pl.when(first & (cx == 0))
    def _():
        for i in range(2):
            dv[i, 0, 0] = zero_plane

        @pl.loop(0, half)
        def _(f):
            for slot in range(2):
                cur[slot][f, 0] = zero_plane

    @pl.when(last & (cx == 1))
    def _():
        @pl.loop(0, half)
        def _(f):
            for slot in range(2):
                cur[slot][f, deep + 1] = zero_plane

    @pl.when(relays)
    def _():
        for a in range(3):
            for block in range(2):
                crossed_faces(a, block).wait_recv()
                relay_faces(a, block).start()
        pl.semaphore_signal(go, inc=1, device_id=sibling, device_id_type=MESH)

    @pl.when(stays)
    def _():
        for i in range(2):
            keep_faces(i).wait()
            give_faces(i, 1 - cx).wait_recv()
        pl.semaphore_wait(go, 1)

    def send_adjoint():
        @pl.loop(EARLY, fields)
        def _(f):
            for ahead in range(1, n_traj):
                gather(ahead, f).start()

    pl.when(relays)(send_adjoint)

    @pl.when(place == 1)
    def _():
        for i in range(2):
            keep_below(i).wait()

    @pl.when((place == 3) | ((cx == 0) & jnp.logical_not(first)))
    def _():
        for i in range(2):
            give_below(i, 0, side_id).wait_recv()

    @pl.when(relays)
    def _():
        for a in range(3):
            for block in range(2):
                relayed_faces(a, block).wait_recv()

    @pl.loop(0, deep)
    def _(zz):
        coefficients(dv, coef, zz)

    def halo_up(slot, c):
        return remote(
            cur[slot].at[pl.ds(c * size, size), deep],
            cur[slot].at[pl.ds(c * size, size), 0],
            up_send.at[slot, c],
            up_recv.at[slot, c],
            above_id,
        )

    def halo_down(slot, c):
        return remote(
            cur[slot].at[pl.ds(c * size, size), 1],
            cur[slot].at[pl.ds(c * size, size), deep + 1],
            down_send.at[slot, c],
            down_recv.at[slot, c],
            below_id,
        )

    def send_halos(slot, c):
        @pl.when(has_up)
        def _():
            halo_up(slot, c).start()

        @pl.when(has_down)
        def _():
            halo_down(slot, c).start()

    def wait_sent(slot, c):
        @pl.when(has_up)
        def _():
            halo_up(slot, c).wait_send()

        @pl.when(has_down)
        def _():
            halo_down(slot, c).wait_send()

    def wait_halos(slot, c):
        @pl.when(has_down)
        def _():
            halo_up(slot, c).wait_recv()

        @pl.when(has_up)
        def _():
            halo_down(slot, c).wait_recv()

    tiles = rows // 8

    def update(slot, c, zs):
        old, new = cur[slot], cur[1 - slot]
        for r in range(tiles):
            at = pl.ds(8 * r, 8)
            for f in [c * size + i for i in range(size)]:
                for zz in zs:
                    k = [coef[i, zz, at] for i in range(7)]
                    p = old[f, zz + 1, at]
                    if r > 0:
                        before = old[f, zz + 1, pl.ds(8 * r - 1, 8)]
                    else:
                        before = pltpu.roll(p, 1, 0)
                    if r < tiles - 1:
                        after = old[f, zz + 1, pl.ds(8 * r + 1, 8)]
                    else:
                        after = pltpu.roll(p, 7, 0)
                    new[f, zz + 1, at] = (
                        k[5] * pltpu.roll(p, lanes - 1, 1)
                        + k[6] * pltpu.roll(p, 1, 1)
                        + k[0] * p
                        + k[1] * old[f, zz + 2, at]
                        + k[2] * old[f, zz, at]
                        + k[3] * after
                        + k[4] * before
                    )

    def add_impulses(c, zz):
        for i in range(size):
            f = c * size + i
            cur0[f, zz + 1] = with_impulse(
                cur0[f, zz + 1],
                src_ref[0, hx * half + f],
                (mine * 2 + cx) * deep + zz,
            )

    def wait_start(c):
        @pl.when(stays)
        def _():
            keep_start(c).wait()
            give_start(c, 1 - cx).wait_recv()

        @pl.when(relays)
        def _():
            for block in range(2):
                cross_start(c, block).wait_recv()

    def keep_final(c):
        return pltpu.make_async_copy(
            cur0.at[pl.ds(c * size, size), own_planes(cx)],
            final.at[chunk_of(hx, c)],
            back_recv.at[c, hx],
        )

    def give_final(c, b, which):
        return remote(
            cur0.at[pl.ds(c * size, size), own_planes(b)],
            final.at[chunk_of(which, c)],
            back_send.at[c, b],
            back_recv.at[c, which],
            {"space": mine * quad + cx * 2 + b},
        )

    @pl.loop(0, steps + 1 + (held - 1) * LAG)
    def _(turn):
        @pl.loop(0, held)
        def _(c):
            t = turn - c * LAG - 1
            pl.when((turn == 1) & (c == 0) & stays)(send_adjoint)

            @pl.when(t == -1)
            def _():
                wait_start(c)
                add_impulses(c, 0)
                add_impulses(c, deep - 1)
                send_halos(0, c)

                @pl.loop(1, deep - 1)
                def _(zz):
                    add_impulses(c, zz)

            for slot in range(2):

                @pl.when((t >= 0) & (t < steps) & (lax.rem(t, 2) == slot))
                def _():
                    @pl.when(t > 0)
                    def _():
                        wait_sent(1 - slot, c)

                    wait_halos(slot, c)

                    update(slot, c, (0, deep - 1))

                    @pl.when(t < steps - 1)
                    def _():
                        send_halos(1 - slot, c)

                    @pl.loop(1, deep - 1, step=2)
                    def _(zz):
                        update(slot, c, (zz, zz + 1))

            @pl.when(t == steps - 1)
            def _():
                @pl.when(stays)
                def _():
                    give_final(c, 1 - cx, hx).start()
                    keep_final(c).start()

                @pl.when(relays)
                def _():
                    for b in range(2):
                        give_final(c, b, hx).start()

    def wait_final(c):
        @pl.when(stays)
        def _():
            keep_final(c).wait()
            give_final(c, 1 - cx, 1 - hx).wait_recv()

        @pl.when(relays)
        def _():
            for which in range(2):
                give_final(c, 0, which).wait_recv()

    def gram_of(c, owner, kb):
        columns = [which * half + c * size + i for which in range(2) for i in range(size)]

        def plane(zz, sums):
            def tile(i, sums):
                at = pl.ds(pl.multiple_of(i * 8, 8), 8)
                left = [a_all[owner, kb * 4 + k, zz, at] for k in range(4)]
                right = [final[j, zz, at] for j in columns]
                return tuple(
                    sums[k * len(columns) + j] + left[k] * right[j]
                    for k in range(4)
                    for j in range(len(columns))
                )

            return lax.fori_loop(0, tiles, tile, sums, unroll=tiles)

        zero = jnp.zeros((8, lanes), jnp.float32)
        sums = lax.fori_loop(0, planes, plane, (zero,) * (4 * len(columns)))
        for k in range(4):
            for j, column in enumerate(columns):
                gred[owner * fields + kb * 4 + k, pl.ds(column, 1)] = jnp.sum(
                    sums[k * len(columns) + j], axis=0, keepdims=True
                )

    blocks = fields // 4

    def gram_own(c):
        @pl.loop(0, blocks)
        def _(kb):
            gram_of(c, my_traj, kb)

    def gram_other(ahead, c, kb):
        gram_of(c, lax.rem(my_traj + n_traj - ahead, n_traj), kb)

    def wait_block(ahead, kb):
        for k in range(4):
            gathered(ahead, kb * 4 + k).wait_recv()

    @pl.loop(0, held - 1)
    def _(c):
        wait_final(c)
        gram_own(c)
        for ahead in range(1, n_traj):

            @pl.loop(0, blocks - 1)
            def _(kb):
                @pl.when(c == 0)
                def _():
                    wait_block(ahead, kb)

                gram_other(ahead, c, kb)

    for ahead in range(1, n_traj):
        wait_block(ahead, blocks - 1)

    @pl.loop(0, held - 1)
    def _(c):
        for ahead in range(1, n_traj):
            gram_other(ahead, c, blocks - 1)

    wait_final(held - 1)
    gram_own(held - 1)
    for ahead in range(1, n_traj):

        @pl.loop(0, blocks)
        def _(kb):
            gram_other(ahead, held - 1, kb)

    stacks = out_ref.shape[0] // 8
    pitch = lanes // stacks
    box[...] = jnp.zeros(box.shape, jnp.float32)
    box[:, pl.ds(0, fields)] = jnp.sum(gred[...], axis=-1)
    packed = box[pl.ds(0, 8)]
    for i in range(1, stacks):
        packed = packed + pltpu.roll(box[pl.ds(8 * i, 8)], pitch * i, 1)
    part[me] = packed

    def share(ahead):
        return remote(
            part.at[me],
            part.at[me],
            red_send.at[ahead - 1],
            red_recv.at[ahead - 1],
            {"space": lax.rem(me + ahead, n)},
        )

    @pl.loop(1, n)
    def _(ahead):
        share(ahead).start()

    @pl.loop(1, n)
    def _(ahead):
        share(ahead).wait_recv()

    value = lax.fori_loop(1, n, lambda i, total: total + part[i], part[0])
    value = value / math.sqrt(n * planes * rows * lanes)
    for i in range(stacks):
        shifted = pltpu.roll(value, (lanes - pitch * i) % lanes, 1) if i else value
        out_ref[pl.ds(8 * i, 8)] = shifted[:, :fields]

    @pl.loop(1, n)
    def _(ahead):
        share(ahead).wait_send()

    @pl.loop(0, fields)
    def _(f):
        for ahead in range(1, n_traj):
            gather(ahead, f).wait_send()

    for a in range(3):
        crossed_faces(a, cx).wait_send()

    @pl.when(place == 1)
    def _():
        for i in range(2):
            give_below(i, 0, side_id).wait_send()

    @pl.when((place == 3) & jnp.logical_not(last))
    def _():
        for i in range(2):
            for k in range(2):
                give_below(i, k, over_id[k]).wait_send()

    @pl.when(relays)
    def _():
        for i in range(2):
            give_faces(i, cx).wait_send()
        for a in range(3):
            for block in range(2):
                relay_faces(a, block).wait_send()

    @pl.loop(0, held)
    def _(c):
        wait_sent(1, c)
        cross_start(c, cx).wait_send()

        @pl.when(stays)
        def _():
            give_final(c, 1 - cx, hx).wait_send()

        @pl.when(relays)
        def _():
            give_start(c, cx).wait_send()
            for b in range(2):
                give_final(c, b, hx).wait_send()


def solution(mesh):
    n, n_traj = mesh.shape["space"], mesh.shape["traj"]

    def on_device(primal_init, adjoint_init, diffusion, velocity, sources):
        fields, planes, rows, lanes = primal_init.shape
        quad = GROUP
        total = n_traj * fields
        assert total % 8 == 0 and fields * total <= 8 * lanes
        assert n % quad == 0 and n_traj % 2 == 0 and fields % (4 * CHUNK) == 0
        size = CHUNK
        half, deep = fields // 2, planes * 2
        held = half // size
        hbm = pl.BlockSpec(memory_space=pltpu.HBM)
        dma = pltpu.SemaphoreType.DMA
        f32 = jnp.float32
        others = max(1, n_traj - 1)
        return pl.pallas_call(
            functools.partial(kernel, (n, n_traj, quad, size)),
            out_shape=jax.ShapeDtypeStruct((total, fields), f32),
            in_specs=[pl.BlockSpec(memory_space=pltpu.SMEM)] + [hbm] * 4,
            out_specs=pl.BlockSpec(memory_space=pltpu.VMEM),
            scratch_shapes=[
                *[pltpu.VMEM((half, deep + 2, rows, lanes), f32)] * 2,
                pltpu.VMEM((fields, planes, rows, lanes), f32),
                pltpu.VMEM((n_traj, fields, planes, rows, lanes), f32),
                pltpu.VMEM((2, 3, deep + 1, rows, lanes), f32),
                pltpu.VMEM((7, deep, rows, lanes), f32),
                pltpu.VMEM((total, fields, lanes), f32),
                pltpu.VMEM((total, lanes), f32),
                pltpu.VMEM((n, 8, lanes), f32),
                dma((fields,)),
                dma((2,)),
                dma((2, 2)),
                dma((3,)),
                *[dma((2, 3))] * 3,
                dma((2, 2)),
                dma((2,)),
                *[dma((others, fields))] * 2,
                *[dma((held, 2))] * 4,
                *[dma((2, held))] * 4,
                *[dma((n - 1,))] * 2,
                pltpu.SemaphoreType.REGULAR,
            ],
            compiler_params=pltpu.CompilerParams(
                collective_id=0, has_side_effects=True, vmem_limit_bytes=67043328
            ),
        )(sources, primal_init, adjoint_init, diffusion, velocity)

    return jax.shard_map(
        on_device,
        mesh=mesh,
        in_specs=(
            P("traj", "space", None, None),
            P("traj", "space", None, None),
            P(None, "space", None, None),
            P(None, "space", None, None),
            P(None, "traj"),
        ),
        out_specs=P(None, "traj"),
        check_vma=False,
    )
```
